512 devices in a mesh: seq: 64 (over z, x, core), head: 8 (over y).
Axes of the slice: x: 4, y: 8, z: 8, core: 2. Of those that a mesh axis runs over, the one named last changes fastest.
Arguments:
- query_proj: bfloat16 [65536, 512], P(('seq', 'head')), may hold values from -4 to 4
- key_proj: bfloat16 [65536, 512], P(('seq', 'head')), may hold values from -8 to 8
- value_proj: bfloat16 [65536, 4096], P(('seq', 'head')), may hold values from -6.5 to 6.5
- conv_query: float32 [3, 512], replicated, may hold values from -1 to 1
- conv_key: float32 [3, 512], replicated, may hold values from -1 to 1
- conv_value: float32 [3, 4096], replicated, may hold values from -1 to 1
Outputs:
- mixed_out: bfloat16 [65536, 4096], P(('seq', 'head'))
The draws below stay inside these ranges and needn't reach their ends.
All inputs are finite; a program needn't handle non-finite values.
Results may differ from the reference program's by a relative error of at most 0.0027.
Values may be sent and summed in bfloat16 or wider, within the bound.
A program may use at most 128 MiB of HBM per device.

```python
import jax
import jax.numpy as jnp
import numpy as np
from jax import lax

H = 32
KD = 16
VD = 128
SPAN = 128
KERNEL = 3
TOK_DEV = 128
FEAT = 153
TOKENS = 65536


def draw_key_proj(key, part):
    position = jnp.arange(TOKENS, dtype=jnp.float32)[:, None]
    gain_rows = 0.5 + 1.5 * position / TOKENS
    noise_part = jnp.clip(jax.random.normal(key, (TOKENS, H * KD), jnp.float32), -4.0, 4.0)
    return (noise_part * gain_rows).astype(jnp.bfloat16)


def draw_value_proj(key, part):
    first_key = jax.random.fold_in(key, 1)
    second_key = jax.random.fold_in(key, 2)
    blocks = TOKENS // TOK_DEV
    offset = jnp.clip(jax.random.normal(second_key, (blocks, H * VD), jnp.float32), -2.5, 2.5)
    offset = jnp.repeat(offset, TOK_DEV, axis=0)
    noise_part = jnp.clip(jax.random.normal(first_key, (TOKENS, H * VD), jnp.float32), -4.0, 4.0)
    return (noise_part + offset).astype(jnp.bfloat16)


def block_levels(own_key, shape, cuts, low, high):
    def one(dim, blocks):
        steps = jax.random.uniform(jax.random.fold_in(jax.random.fold_in(own_key, 6), dim), (blocks,), jnp.float32, low / len(cuts), high / len(cuts))
        return jnp.repeat(jnp.exp(steps), shape[dim] // blocks).reshape((-1,) + (1,) * (len(shape) - dim - 1))

    loudness = one(*cuts[0])
    for cut in cuts[1:]:
        loudness = loudness * one(*cut)
    return loudness


def scatter_about(stream_key, dims, width, limit, cuts=(), kind=jnp.bfloat16):
    result = width * jax.random.normal(stream_key, dims, jnp.float32)
    if cuts:
        result = result * block_levels(stream_key, dims, cuts, -0.22, 0.18)
    return jnp.clip(result, -limit, limit).astype(kind)


def setup_inputs(seed: int = 0) -> dict:
    streams_of = jax.random.split(jax.random.key(seed), 7)
    query_proj = scatter_about(streams_of[0], (TOKENS, H * KD), 1.0, 4.0, ((0, 512),))
    key_proj = draw_key_proj(jax.random.fold_in(streams_of[6], 71), 0)
    value_proj = draw_value_proj(jax.random.fold_in(streams_of[6], 71), 0)
    conv_query = jnp.clip(jax.random.uniform(streams_of[3], (KERNEL, H * KD), jnp.float32, -1.0, 1.0), -1.0, 1.0)
    conv_key = jnp.clip(jax.random.uniform(streams_of[4], (KERNEL, H * KD), jnp.float32, -1.0, 1.0), -1.0, 1.0)
    conv_value = jnp.clip(jax.random.uniform(streams_of[5], (KERNEL, H * VD), jnp.float32, -1.0, 1.0), -1.0, 1.0)
    return {"query_proj": query_proj, "key_proj": key_proj, "value_proj": value_proj, "conv_query": conv_query, "conv_key": conv_key, "conv_value": conv_value}


def features(values):
    scaled = values * (KD ** -0.25)
    first_index, second_index = np.triu_indices(KD, 1)
    cross = scaled[..., first_index] * scaled[..., second_index]
    return jnp.concatenate([jnp.ones_like(scaled[..., :1]), scaled, scaled * scaled * (0.5 ** 0.5), cross], axis=-1)


def convolve(row_block, tap_rows):
    length = row_block.shape[0]
    summed = jnp.zeros(row_block.shape, jnp.float32)
    for offset in range(KERNEL):
        shifted = jnp.pad(row_block, ((offset, 0), (0, 0)))[:length]
        summed = summed + tap_rows[offset] * shifted
    return summed


def reference(query_proj, key_proj, value_proj, conv_query, conv_key, conv_value):
    query_conv = convolve(query_proj.astype(jnp.float32), conv_query)
    key_conv = convolve(key_proj.astype(jnp.float32), conv_key)
    value_conv = convolve(value_proj.astype(jnp.float32), conv_value).astype(jnp.bfloat16)
    length = query_conv.shape[0]
    block_count = length // SPAN
    query_heads = query_conv.reshape(length, H, KD).transpose(1, 0, 2)
    key_heads = key_conv.reshape(length, H, KD).transpose(1, 0, 2)
    value_heads = value_conv.reshape(length, H, VD).transpose(1, 0, 2)
    causal = jnp.arange(SPAN)[:, None] >= jnp.arange(SPAN)[None, :]

    def one_head(operands):
        query_rows, key_rows, value_rows = operands
        query_feat = lax.optimization_barrier(features(query_rows).astype(jnp.bfloat16))
        key_feat = lax.optimization_barrier(features(key_rows).astype(jnp.bfloat16))
        query_float = query_feat.astype(jnp.float32).reshape(block_count, SPAN, FEAT)
        key_float = key_feat.astype(jnp.float32).reshape(block_count, SPAN, FEAT)
        value_float = value_rows.astype(jnp.float32).reshape(block_count, SPAN, VD)
        scores = jnp.einsum('ncf,nmf->ncm', query_float, key_float)
        scores = jnp.where(causal, scores, jnp.float32(0.0))
        inner_den = jnp.sum(scores, axis=-1)
        rounded = lax.optimization_barrier(scores.astype(jnp.bfloat16))
        inner_num = jnp.einsum('ncm,nmv->ncv', rounded.astype(jnp.float32), value_float)
        block_state = jnp.einsum('nmf,nmv->nfv', key_float, value_float)
        block_norm = jnp.sum(key_float, axis=1)
        prefix_state = jnp.concatenate([jnp.zeros_like(block_state[:1]), jnp.cumsum(block_state, axis=0)[:-1]], axis=0)
        prefix_norm = jnp.concatenate([jnp.zeros_like(block_norm[:1]), jnp.cumsum(block_norm, axis=0)[:-1]], axis=0)
        numerator = inner_num + jnp.einsum('ncf,nfv->ncv', query_float, prefix_state, precision=lax.Precision.HIGHEST)
        denominator = inner_den + jnp.einsum('ncf,nf->nc', query_float, prefix_norm, precision=lax.Precision.HIGHEST)
        return (numerator / denominator[..., None]).astype(jnp.bfloat16).reshape(length, VD)

    mixed_heads = lax.map(one_head, (query_heads, key_heads, value_heads))
    return mixed_heads.transpose(1, 0, 2).reshape(length, H * VD)
```

```python
import functools

import jax
import jax.numpy as jnp
from jax import lax
from jax.experimental import pallas as pl
from jax.experimental.pallas import tpu as pltpu
from jax.sharding import PartitionSpec as P

KD = 16
VD = 128
SPAN = 128
KERNEL = 3
HALO = 16
FEAT = 160
PLANE = 8
MESH = pl.DeviceIdType.MESH


def features(rows):
    parts = [rows, rows * rows * (0.5**0.5)]
    for step in range(1, KD // 2):
        parts.append(rows * jnp.concatenate([rows[step:], rows[:step]], axis=0))
    parts.append(rows[: KD // 2] * rows[KD // 2 :])
    index = lax.broadcasted_iota(jnp.int32, (8, rows.shape[1]), 0)
    parts.append(jnp.where(index == 0, 1.0, 0.0).astype(jnp.float32))
    return jnp.concatenate(parts, axis=0)


def convolve(block, before, taps):
    row = lax.broadcasted_iota(jnp.int32, block.shape, 0)
    last = before[HALO - 1 : HALO]
    second = before[HALO - 2 : HALO - 1]
    one = jnp.where(row == 0, last, pltpu.roll(block, 1, 0))
    two = jnp.where(row == 0, second, jnp.where(row == 1, last, pltpu.roll(block, 2, 0)))
    return taps[0:1] * block + taps[1:2] * one + taps[2:3] * two


def split(value):
    high = value.astype(jnp.bfloat16)
    return high, (value - high.astype(jnp.float32)).astype(jnp.bfloat16)


def dot(a, b):
    return jnp.dot(a, b, preferred_element_type=jnp.float32)


def kernel(
    shards,
    groups,
    heads,
    qk_hbm,
    v_hbm,
    taps_qk,
    taps_v,
    out_hbm,
    qk_in,
    v_in,
    key_feat,
    query_feat,
    value,
    before_state,
    numer,
    denom,
    total,
    slices,
    plane,
    others,
    carried,
    prefixes,
    carry,
    result,
    qk_send,
    qk_recv,
    v_send,
    v_recv,
    halo_send,
    halo_recv,
    one_send,
    one_recv,
    two_send,
    two_recv,
    three_send,
    three_recv,
    out_send,
    out_recv,
    own_sem,
):
    s = lax.axis_index("seq")
    y = lax.axis_index("head")
    z = s // PLANE
    r = s % PLANE
    layers = shards // PLANE
    width = heads * VD
    part = slices.shape[1]

    def y_peer(step):
        return (y + step) % groups

    def r_peer(step):
        return (r + step) % PLANE

    following = (s + 1) % shards
    preceding = (s + shards - 1) % shards

    barrier = pltpu.get_barrier_semaphore()
    greet = [(s, y_peer(d)) for d in range(1, groups)]
    greet += [(z * PLANE + r_peer(d), y) for d in range(1, PLANE)]
    greet += [(((z + d) % layers) * PLANE + r, y) for d in range(1, layers)]
    greet += [(following, y), (preceding, y)]
    for place in greet:
        pl.semaphore_signal(barrier, inc=1, device_id=place, device_id_type=MESH)
    pl.semaphore_wait(barrier, len(greet))

    def columns(group):
        return pl.ds(pl.multiple_of(group * width, width), width)

    def remote(src, dst, send, recv, place):
        return pltpu.make_async_remote_copy(
            src_ref=src,
            dst_ref=dst,
            send_sem=send,
            recv_sem=recv,
            device_id=place,
            device_id_type=MESH,
        )

    def send_qk(peer, owner, semaphore):
        return remote(
            qk_hbm.at[peer], qk_in.at[owner + 1], qk_send.at[peer], qk_recv.at[semaphore], (s, peer)
        )

    def send_v(peer, owner, semaphore):
        return remote(
            v_hbm.at[:, columns(peer)],
            v_in.at[owner + 1],
            v_send.at[peer],
            v_recv.at[semaphore],
            (s, peer),
        )

    for d in range(1, groups):
        send_qk(y_peer(d), y, y).start()
    for d in range(1, groups):
        send_v(y_peer(d), y, y).start()
    own_qk = pltpu.make_async_copy(qk_hbm.at[y], qk_in.at[y + 1], own_sem.at[0])
    own_v = pltpu.make_async_copy(v_hbm.at[:, columns(y)], v_in.at[y + 1], own_sem.at[1])
    own_qk.start()
    own_v.start()
    own_qk.wait()
    own_v.wait()
    for d in range(1, groups):
        send_qk(y_peer(d), y_peer(d), y_peer(d)).wait_recv()
    for d in range(1, groups):
        send_v(y_peer(d), y_peer(d), y_peer(d)).wait_recv()

    tail = pl.ds(SPAN - HALO, HALO)
    halo_qk = remote(
        qk_in.at[groups, tail],
        qk_in.at[0, tail],
        halo_send.at[0],
        halo_recv.at[0],
        (following, y),
    )
    halo_v = remote(
        v_in.at[groups, tail], v_in.at[0, tail], halo_send.at[1], halo_recv.at[1], (following, y)
    )
    halo_qk.start()
    halo_v.start()
    halo_qk.wait()
    halo_v.wait()

    total[...] = jnp.zeros_like(total)
    lane = lax.broadcasted_iota(jnp.int32, (FEAT, VD), 1)

    def summarize(n, _):
        keep = jnp.logical_or(n > 0, s > 0)
        qk_before = jnp.where(keep, qk_in[n, SPAN - HALO :].astype(jnp.float32), 0.0)
        v_before = jnp.where(keep, v_in[n, SPAN - HALO :].astype(jnp.float32), 0.0)
        qk = convolve(qk_in[n + 1].astype(jnp.float32), qk_before, taps_qk[y])
        rows = (qk * KD**-0.25).T
        mixed = convolve(v_in[n + 1].astype(jnp.float32), v_before, taps_v[:, columns(y)])
        mixed = mixed.astype(jnp.bfloat16)
        norms = total[heads * FEAT : (heads + 1) * FEAT]
        for h in range(heads):
            query = features(rows[h * KD : (h + 1) * KD])
            key = features(rows[(heads + h) * KD : (heads + h + 1) * KD]).astype(jnp.bfloat16)
            own = mixed[:, h * VD : (h + 1) * VD]
            query_feat[h, n] = query.T.astype(jnp.bfloat16)
            key_feat[h, n] = key
            value[h, n] = own
            both = jnp.concatenate([own, jnp.ones_like(own)], axis=1)
            added = dot(key, both)
            state = total[h * FEAT : (h + 1) * FEAT]
            before_state[h, n, :, :VD] = state
            before_state[h, n, :, VD:] = jnp.broadcast_to(
                norms[:, h * 32 : h * 32 + 1], (FEAT, VD)
            )
            total[h * FEAT : (h + 1) * FEAT] = state + added[:, :VD]
            norms = norms + jnp.where(lane // 32 == h, added[:, VD:], 0.0)
        total[heads * FEAT : (heads + 1) * FEAT] = norms
        return 0

    lax.fori_loop(0, groups, summarize, 0)

    def piece(ref, index):
        return ref.at[pl.ds(pl.multiple_of(index * part, 8), part)]

    def send_one(peer, owner):
        return remote(
            piece(total, peer),
            slices.at[owner],
            one_send.at[peer],
            one_recv.at[owner],
            (z * PLANE + peer, y),
        )

    for d in range(1, PLANE):
        send_one(r_peer(d), r).start()
    slices[r] = total[pl.ds(pl.multiple_of(r * part, 8), part)]

    causal = lax.broadcasted_iota(jnp.int32, (SPAN, SPAN), 0) >= lax.broadcasted_iota(
        jnp.int32, (SPAN, SPAN), 1
    )

    def attend(h):
        def one(n, _):
            query = query_feat[h, n]
            scores = jnp.where(causal, dot(query, key_feat[h, n]), 0.0)
            high, low = split(before_state[h, n])
            earlier = dot(query, high) + dot(query, low)
            numer[h, n] = dot(scores.astype(jnp.bfloat16), value[h, n]) + earlier[:, :VD]
            denom[h, n] = jnp.sum(scores, axis=1, keepdims=True) + earlier[:, VD:]
            return 0

        lax.fori_loop(0, groups, one, 0)

    attend(0)
    attend(1)

    for d in range(1, PLANE):
        send_one(r_peer(d), r_peer(d)).wait_recv()
    running = slices[0]
    for other in range(1, PLANE):
        running = running + slices[other]
    plane[...] = running

    def send_two(to, owner):
        return remote(
            plane, others.at[owner], two_send.at[to], two_recv.at[owner], (to * PLANE + r, y)
        )

    for to in range(1, layers):

        @pl.when(z < to)
        def _():
            send_two(to, z).start()

    attend(2)

    carried[...] = jnp.zeros_like(carried)
    for owner in range(layers - 1):

        @pl.when(owner < z)
        def _():
            send_two(z, owner).wait_recv()
            carried[...] += others[owner]

    running = carried[...]
    prefixes[0] = running
    for other in range(1, PLANE):
        running = running + slices[other - 1]
        prefixes[other] = running

    def send_three(peer, owner):
        return remote(
            prefixes.at[peer],
            piece(carry, owner),
            three_send.at[peer],
            three_recv.at[owner],
            (z * PLANE + peer, y),
        )

    for d in range(1, PLANE):
        send_three(r_peer(d), r).start()
    carry[pl.ds(pl.multiple_of(r * part, 8), part)] = prefixes[r]

    for h in range(3, heads):
        attend(h)

    for d in range(1, PLANE):
        send_three(r_peer(d), r_peer(d)).wait_recv()

    def send_out(peer, owner):
        return remote(
            result.at[peer],
            out_hbm.at[:, columns(owner)],
            out_send.at[peer],
            out_recv.at[owner],
            (s, peer),
        )

    carry_parts = []
    for h in range(heads):
        column = carry[heads * FEAT : (heads + 1) * FEAT][:, h * 32 : h * 32 + 1]
        both = jnp.concatenate(
            [carry[h * FEAT : (h + 1) * FEAT], jnp.broadcast_to(column, (FEAT, VD))], axis=1
        )
        high, low = split(both)
        carry_parts.append((high, low))

    def finish(n):
        for h in range(heads):
            query = query_feat[h, n]
            earlier = dot(query, carry_parts[h][0]) + dot(query, carry_parts[h][1])
            mixed = (numer[h, n] + earlier[:, :VD]) / (denom[h, n] + earlier[:, VD:])
            result[n, :, h * VD : (h + 1) * VD] = mixed.astype(jnp.bfloat16)

    def finish_and_send(step, _):
        peer = y_peer(step)
        finish(peer)
        send_out(peer, y).start()
        return 0

    lax.fori_loop(1, groups, finish_and_send, 0)
    finish(y)
    own_out = pltpu.make_async_copy(result.at[y], out_hbm.at[:, columns(y)], own_sem.at[2])
    own_out.start()

    for d in range(1, groups):
        send_qk(y_peer(d), y, y).wait_send()
        send_v(y_peer(d), y, y).wait_send()
    for d in range(1, PLANE):
        send_one(r_peer(d), r).wait_send()
        send_three(r_peer(d), r).wait_send()
    for to in range(1, layers):

        @pl.when(z < to)
        def _():
            send_two(to, z).wait_send()

    own_out.wait()
    for d in range(1, groups):
        send_out(y_peer(d), y).wait_send()
        send_out(y_peer(d), y_peer(d)).wait_recv()


def on_device(shards, groups, query_proj, key_proj, value_proj, conv_query, conv_key, conv_value):
    tokens = query_proj.shape[0]
    heads = query_proj.shape[1] // KD // groups

    def grouped(query, key):
        rows = query.shape[0]
        both = jnp.concatenate(
            [query.reshape(rows, groups, heads * KD), key.reshape(rows, groups, heads * KD)],
            axis=2,
        )
        return both.transpose(1, 0, 2)

    qk = grouped(query_proj, key_proj)
    taps_qk = grouped(conv_query, conv_key)
    rows = (heads + 1) * FEAT
    part = -(-rows // (8 * PLANE)) * 8
    layers = shards // PLANE
    scratch = pltpu.VMEM
    dma = pltpu.SemaphoreType.DMA
    f32, bf16 = jnp.float32, jnp.bfloat16
    return pl.pallas_call(
        functools.partial(kernel, shards, groups, heads),
        out_shape=jax.ShapeDtypeStruct(value_proj.shape, bf16),
        in_specs=[
            pl.BlockSpec(memory_space=pl.ANY),
            pl.BlockSpec(memory_space=pl.ANY),
            pl.BlockSpec(memory_space=pltpu.VMEM),
            pl.BlockSpec(memory_space=pltpu.VMEM),
        ],
        out_specs=pl.BlockSpec(memory_space=pl.ANY),
        scratch_shapes=[
            scratch((groups + 1, tokens, 2 * heads * KD), bf16),
            scratch((groups + 1, tokens, heads * VD), bf16),
            scratch((heads, groups, FEAT, SPAN), bf16),
            scratch((heads, groups, SPAN, FEAT), bf16),
            scratch((heads, groups, SPAN, VD), bf16),
            scratch((heads, groups, FEAT, 2 * VD), f32),
            scratch((heads, groups, SPAN, VD), f32),
            scratch((heads, groups, SPAN, VD), f32),
            scratch((part * PLANE, VD), f32),
            scratch((PLANE, part, VD), f32),
            scratch((part, VD), f32),
            scratch((layers, part, VD), f32),
            scratch((part, VD), f32),
            scratch((PLANE, part, VD), f32),
            scratch((part * PLANE, VD), f32),
            scratch((groups, tokens, heads * VD), bf16),
            dma((groups,)),
            dma((groups,)),
            dma((groups,)),
            dma((groups,)),
            dma((2,)),
            dma((2,)),
            dma((PLANE,)),
            dma((PLANE,)),
            dma((layers,)),
            dma((layers,)),
            dma((PLANE,)),
            dma((PLANE,)),
            dma((groups,)),
            dma((groups,)),
            dma((3,)),
        ],
        compiler_params=pltpu.CompilerParams(collective_id=0, has_side_effects=True),
    )(qk, value_proj, taps_qk, conv_value)


def solution(mesh):
    shards, groups = mesh.shape["seq"], mesh.shape["head"]
    rows = P(("seq", "head"), None)
    return jax.shard_map(
        functools.partial(on_device, shards, groups),
        mesh=mesh,
        in_specs=(rows, rows, rows, P(), P(), P()),
        out_specs=rows,
        check_vma=False,
    )
```

```python
import functools

import jax
import jax.numpy as jnp
from jax import lax
from jax.experimental import pallas as pl
from jax.experimental.pallas import tpu as pltpu
from jax.sharding import PartitionSpec as P

KD = 16
VD = 128
SPAN = 128
KERNEL = 3
HALO = 16
FEAT = 160
PLANE = 8
MESH = pl.DeviceIdType.MESH


def features(rows):
    parts = [rows, rows * rows * (0.5**0.5)]
    for step in range(1, KD // 2):
        parts.append(rows * jnp.concatenate([rows[step:], rows[:step]], axis=0))
    parts.append(rows[: KD // 2] * rows[KD // 2 :])
    index = lax.broadcasted_iota(jnp.int32, (8, rows.shape[1]), 0)
    parts.append(jnp.where(index == 0, 1.0, 0.0).astype(jnp.float32))
    return jnp.concatenate(parts, axis=0)


def convolve(block, before, taps):
    row = lax.broadcasted_iota(jnp.int32, block.shape, 0)
    last = before[HALO - 1 : HALO]
    second = before[HALO - 2 : HALO - 1]
    one = jnp.where(row == 0, last, pltpu.roll(block, 1, 0))
    two = jnp.where(row == 0, second, jnp.where(row == 1, last, pltpu.roll(block, 2, 0)))
    return taps[0:1] * block + taps[1:2] * one + taps[2:3] * two


def split(value):
    high = value.astype(jnp.bfloat16)
    return high, (value - high.astype(jnp.float32)).astype(jnp.bfloat16)


def dot(a, b):
    return jnp.dot(a, b, preferred_element_type=jnp.float32)


def kernel(
    shards,
    groups,
    heads,
    query_ref,
    key_ref,
    v_hbm,
    taps_query,
    taps_key,
    taps_v,
    out_hbm,
    qk_out,
    qk_in,
    v_in,
    v_halo,
    taps_qk,
    key_feat,
    query_feat,
    value,
    before_state,
    numer,
    denom,
    total,
    slices,
    plane,
    others,
    carried,
    prefixes,
    carry,
    result,
    qk_send,
    qk_recv,
    v_send,
    v_recv,
    halo_send,
    halo_recv,
    one_send,
    one_recv,
    two_send,
    two_recv,
    three_send,
    three_recv,
    out_send,
    out_recv,
    own_qk_sem,
    own_v_sem,
    own_out_sem,
):
    s = lax.axis_index("seq")
    y = lax.axis_index("head")
    z = s // PLANE
    r = s % PLANE
    layers = shards // PLANE
    last = groups - 1
    near = heads * KD

    def y_peer(step):
        return (y + step) % groups

    def r_peer(step):
        return (r + step) % PLANE

    following = (s + 1) % shards
    preceding = (s + shards - 1) % shards
    order = sorted(range(1, groups), key=lambda step: min(step, groups - step))

    barrier = pltpu.get_barrier_semaphore()
    greet = [(s, y_peer(d)) for d in order]
    greet += [(z * PLANE + r_peer(d), y) for d in range(1, PLANE)]
    greet += [(((z + d) % layers) * PLANE + r, y) for d in range(1, layers)]
    for place in greet + [(preceding, last)]:
        pl.semaphore_signal(barrier, inc=1, device_id=place, device_id_type=MESH)

    for g in range(groups):
        own = slice(g * near, (g + 1) * near)
        qk_out[g] = jnp.concatenate([query_ref[:, own], key_ref[:, own]], axis=1)
        taps_qk[g, :KERNEL] = jnp.concatenate([taps_query[:, own], taps_key[:, own]], axis=1)

    @pl.when(y == last)
    def _():
        pl.semaphore_wait(barrier, len(greet) + groups)

    @pl.when(y != last)
    def _():
        pl.semaphore_wait(barrier, len(greet))

    def columns(group, h):
        return pl.ds(pl.multiple_of((group * heads + h) * VD, VD), VD)

    def wide(group):
        return pl.ds(pl.multiple_of(group * heads * VD, heads * VD), heads * VD)

    def remote(src, dst, send, recv, place):
        return pltpu.make_async_remote_copy(
            src_ref=src,
            dst_ref=dst,
            send_sem=send,
            recv_sem=recv,
            device_id=place,
            device_id_type=MESH,
        )

    tail = pl.ds(SPAN - HALO, HALO)

    def send_halo_qk(group):
        return remote(
            qk_out.at[group, tail],
            qk_in.at[0, tail],
            halo_send.at[0, group],
            halo_recv.at[0],
            (following, group),
        )

    def send_halo_v(group):
        return remote(
            v_hbm.at[tail, wide(group)],
            v_halo,
            halo_send.at[1, group],
            halo_recv.at[1],
            (following, group),
        )

    def send_qk(peer, owner):
        return remote(
            qk_out.at[peer], qk_in.at[owner + 1], qk_send.at[peer], qk_recv.at[owner], (s, peer)
        )

    def send_v(h, peer, owner):
        return remote(
            v_hbm.at[:, columns(peer, h)],
            v_in.at[h, owner],
            v_send.at[h, peer],
            v_recv.at[h, owner],
            (s, peer),
        )

    def own_v(h):
        return pltpu.make_async_copy(v_hbm.at[:, columns(y, h)], v_in.at[h, y], own_v_sem.at[h])

    own_qk = pltpu.make_async_copy(qk_out.at[y], qk_in.at[y + 1], own_qk_sem.at[0])
    for d in order:
        send_qk(y_peer(d), y).start()

    @pl.when(y == last)
    def _():
        for group in range(groups):
            send_halo_qk(group).start()
            send_halo_v(group).start()

    own_qk.start()
    for h in range(heads):
        for d in order:
            send_v(h, y_peer(d), y).start()
        own_v(h).start()

    total[...] = jnp.zeros_like(total)
    own_qk.wait()
    for d in order:
        send_qk(y_peer(d), y_peer(d)).wait_recv()
    send_halo_qk(y).wait_recv()

    def expand(n, _):
        keep = jnp.logical_or(n > 0, s > 0)
        before = jnp.where(keep, qk_in[n, SPAN - HALO :].astype(jnp.float32), 0.0)
        qk = convolve(qk_in[n + 1].astype(jnp.float32), before, taps_qk[y, :KERNEL])
        rows = (qk * KD**-0.25).T
        for h in range(heads):
            query = features(rows[h * KD : (h + 1) * KD])
            key = features(rows[near + h * KD : near + (h + 1) * KD])
            query_feat[h, n] = query.T.astype(jnp.bfloat16)
            key_feat[h, n] = key.astype(jnp.bfloat16)
        return 0

    lax.fori_loop(0, groups, expand, 0)
    send_halo_v(y).wait_recv()

    def summarize(h):
        own_v(h).wait()
        for d in order:
            send_v(h, y_peer(d), y_peer(d)).wait_recv()
        taps = taps_v[:, columns(y, h)]
        state = jnp.zeros((FEAT, 2 * VD), jnp.float32)
        for n in range(groups):
            if n == 0:
                before = v_halo[:, pl.ds(pl.multiple_of(h * VD, VD), VD)].astype(jnp.float32)
                before = jnp.where(s > 0, before, 0.0)
            else:
                before = v_in[h, n - 1, SPAN - HALO :].astype(jnp.float32)
            own = convolve(v_in[h, n].astype(jnp.float32), before, taps).astype(jnp.bfloat16)
            value[h, n] = own
            before_state[h, n] = state
            both = jnp.concatenate([own, jnp.ones_like(own)], axis=1)
            state = state + dot(key_feat[h, n], both)
        norm = state[:, VD:].T[:8]
        total[h, :FEAT] = state[:, :VD]
        total[h, FEAT : FEAT + 8] = norm[:, :VD]
        total[h, FEAT + 8 : FEAT + 16, : FEAT - VD] = norm[:, VD:]

    part = total.shape[1] // PLANE

    def piece(index):
        return pl.ds(pl.multiple_of(index * part, 8), part)

    def send_one(h, peer, owner):
        return remote(
            total.at[h, piece(peer)],
            slices.at[h, owner],
            one_send.at[h, peer],
            one_recv.at[h, owner],
            (z * PLANE + peer, y),
        )

    def start_one(h):
        for d in range(1, PLANE):
            send_one(h, r_peer(d), r).start()
        slices[h, r] = total[h, piece(r)]

    def send_two(h, to, owner):
        return remote(
            plane.at[h],
            others.at[h, owner],
            two_send.at[h, to],
            two_recv.at[h, owner],
            (to * PLANE + r, y),
        )

    def start_two(h):
        for d in range(1, PLANE):
            send_one(h, r_peer(d), r_peer(d)).wait_recv()
        running = slices[h, 0]
        for other in range(1, PLANE):
            running = running + slices[h, other]
        plane[h] = running
        for to in range(1, layers):

            @pl.when(z < to)
            def _():
                send_two(h, to, z).start()

    def send_three(h, peer, owner):
        return remote(
            prefixes.at[h, peer],
            carry.at[h, piece(owner)],
            three_send.at[h, peer],
            three_recv.at[h, owner],
            (z * PLANE + peer, y),
        )

    def start_three(h):
        carried[...] = jnp.zeros_like(carried)
        for owner in range(layers - 1):

            @pl.when(owner < z)
            def _():
                send_two(h, z, owner).wait_recv()
                carried[...] += others[h, owner]

        running = carried[...]
        prefixes[h, 0] = running
        for other in range(1, PLANE):
            running = running + slices[h, other - 1]
            prefixes[h, other] = running
        for d in range(1, PLANE):
            send_three(h, r_peer(d), r).start()
        carry[h, piece(r)] = prefixes[h, r]

    causal = lax.broadcasted_iota(jnp.int32, (SPAN, SPAN), 0) >= lax.broadcasted_iota(
        jnp.int32, (SPAN, SPAN), 1
    )

    def attend(h):
        for n in range(groups):
            query = query_feat[h, n]
            scores = jnp.where(causal, dot(query, key_feat[h, n]), 0.0)
            high, low = split(before_state[h, n])
            earlier = dot(query, high) + dot(query, low)
            numer[h, n] = dot(scores.astype(jnp.bfloat16), value[h, n]) + earlier[:, :VD]
            denom[h, n] = jnp.sum(scores, axis=1, keepdims=True) + earlier[:, VD:]

    def send_out(h, peer, owner):
        return remote(
            result.at[h, peer],
            out_hbm.at[:, columns(owner, h)],
            out_send.at[h, peer],
            out_recv.at[h, owner],
            (s, peer),
        )

    def own_out(h):
        return pltpu.make_async_copy(
            result.at[h, y], out_hbm.at[:, columns(y, h)], own_out_sem.at[h]
        )

    def finish(h):
        for d in range(1, PLANE):
            send_three(h, r_peer(d), r_peer(d)).wait_recv()
        norm = jnp.concatenate(
            [carry[h, FEAT : FEAT + 8], carry[h, FEAT + 8 : FEAT + 16][:, : FEAT - VD]], axis=1
        )
        norm = jnp.broadcast_to(norm[:1], (VD, FEAT)).T
        high, low = split(jnp.concatenate([carry[h, :FEAT], norm], axis=1))
        for d in order + [0]:
            n = y_peer(d)
            query = query_feat[h, n]
            earlier = dot(query, high) + dot(query, low)
            mixed = (numer[h, n] + earlier[:, :VD]) / (denom[h, n] + earlier[:, VD:])
            result[h, n] = mixed.astype(jnp.bfloat16)
            if d:
                send_out(h, n, y).start()
        own_out(h).start()

    summarize(0)
    start_one(0)
    attend(0)
    start_two(0)

    def one_head(h, _):
        summarize(h)
        start_one(h)
        start_three(h - 1)
        attend(h)
        start_two(h)
        finish(h - 1)
        return 0

    lax.fori_loop(1, heads, one_head, 0)
    start_three(heads - 1)
    finish(heads - 1)

    for d in order:
        send_qk(y_peer(d), y).wait_send()

    @pl.when(y == last)
    def _():
        for group in range(groups):
            send_halo_qk(group).wait_send()
            send_halo_v(group).wait_send()

    def drain(h, _):
        for d in order:
            send_v(h, y_peer(d), y).wait_send()
        for d in range(1, PLANE):
            send_one(h, r_peer(d), r).wait_send()
            send_three(h, r_peer(d), r).wait_send()
        for to in range(1, layers):

            @pl.when(z < to)
            def _():
                send_two(h, to, z).wait_send()

        own_out(h).wait()
        for d in order:
            send_out(h, y_peer(d), y).wait_send()
            send_out(h, y_peer(d), y_peer(d)).wait_recv()
        return 0

    lax.fori_loop(0, heads, drain, 0)


def on_device(shards, groups, query_proj, key_proj, value_proj, conv_query, conv_key, conv_value):
    tokens = query_proj.shape[0]
    heads = query_proj.shape[1] // KD // groups
    rows = -(-(FEAT + 16) // (8 * PLANE)) * 8 * PLANE
    part = rows // PLANE
    layers = shards // PLANE
    scratch = pltpu.VMEM
    dma = pltpu.SemaphoreType.DMA
    f32, bf16 = jnp.float32, jnp.bfloat16
    whole = pl.BlockSpec(memory_space=pltpu.VMEM)
    return pl.pallas_call(
        functools.partial(kernel, shards, groups, heads),
        out_shape=jax.ShapeDtypeStruct(value_proj.shape, bf16),
        in_specs=[whole, whole, pl.BlockSpec(memory_space=pl.ANY), whole, whole, whole],
        out_specs=pl.BlockSpec(memory_space=pl.ANY),
        scratch_shapes=[
            scratch((groups, tokens, 2 * heads * KD), bf16),
            scratch((groups + 1, tokens, 2 * heads * KD), bf16),
            scratch((heads, groups, tokens, VD), bf16),
            scratch((HALO, heads * VD), bf16),
            scratch((groups, 8, 2 * heads * KD), f32),
            scratch((heads, groups, FEAT, SPAN), bf16),
            scratch((heads, groups, SPAN, FEAT), bf16),
            scratch((heads, groups, SPAN, VD), bf16),
            scratch((heads, groups, FEAT, 2 * VD), f32),
            scratch((heads, groups, SPAN, VD), f32),
            scratch((heads, groups, SPAN, VD), f32),
            scratch((heads, rows, VD), f32),
            scratch((heads, PLANE, part, VD), f32),
            scratch((heads, part, VD), f32),
            scratch((heads, layers, part, VD), f32),
            scratch((part, VD), f32),
            scratch((heads, PLANE, part, VD), f32),
            scratch((heads, rows, VD), f32),
            scratch((heads, groups, tokens, VD), bf16),
            dma((groups,)),
            dma((groups,)),
            dma((heads, groups)),
            dma((heads, groups)),
            dma((2, groups)),
            dma((2,)),
            dma((heads, PLANE)),
            dma((heads, PLANE)),
            dma((heads, layers)),
            dma((heads, layers)),
            dma((heads, PLANE)),
            dma((heads, PLANE)),
            dma((heads, groups)),
            dma((heads, groups)),
            dma((1,)),
            dma((heads,)),
            dma((heads,)),
        ],
        compiler_params=pltpu.CompilerParams(collective_id=0, has_side_effects=True),
    )(query_proj, key_proj, value_proj, conv_query, conv_key, conv_value)


def solution(mesh):
    shards, groups = mesh.shape["seq"], mesh.shape["head"]
    rows = P(("seq", "head"), None)
    return jax.shard_map(
        functools.partial(on_device, shards, groups),
        mesh=mesh,
        in_specs=(rows, rows, rows, P(), P(), P()),
        out_specs=rows,
        check_vma=False,
    )
```

```python
import functools

import jax
import jax.numpy as jnp
from jax import lax
from jax.experimental import pallas as pl
from jax.experimental.pallas import tpu as pltpu
from jax.sharding import PartitionSpec as P

KD = 16
VD = 128
SPAN = 128
KERNEL = 3
HALO = 16
FEAT = 160
PLANE = 8
MESH = pl.DeviceIdType.MESH


def features(rows):
    parts = [rows, rows * rows * (0.5**0.5)]
    for step in range(1, KD // 2):
        parts.append(rows * jnp.concatenate([rows[step:], rows[:step]], axis=0))
    parts.append(rows[: KD // 2] * rows[KD // 2 :])
    index = lax.broadcasted_iota(jnp.int32, (8, rows.shape[1]), 0)
    parts.append(jnp.where(index == 0, 1.0, 0.0).astype(jnp.float32))
    return jnp.concatenate(parts, axis=0)


def convolve(block, before, taps):
    row = lax.broadcasted_iota(jnp.int32, block.shape, 0)
    last = before[HALO - 1 : HALO]
    second = before[HALO - 2 : HALO - 1]
    one = jnp.where(row == 0, last, pltpu.roll(block, 1, 0))
    two = jnp.where(row == 0, second, jnp.where(row == 1, last, pltpu.roll(block, 2, 0)))
    return taps[0:1] * block + taps[1:2] * one + taps[2:3] * two


def split(value):
    high = value.astype(jnp.bfloat16)
    return high, (value - high.astype(jnp.float32)).astype(jnp.bfloat16)


def dot(a, b):
    return jnp.dot(a, b, preferred_element_type=jnp.float32)


def kernel(
    shards,
    groups,
    heads,
    query_ref,
    key_ref,
    v_hbm,
    taps_query,
    taps_key,
    taps_v,
    out_ref,
    qk_out,
    qk_in,
    v_in,
    v_halo,
    taps_qk,
    key_feat,
    query_feat,
    value,
    before_state,
    numer,
    denom,
    total,
    slices,
    plane,
    others,
    carried,
    prefixes,
    carry,
    result,
    qk_send,
    qk_recv,
    v_send,
    v_recv,
    halo_send,
    halo_recv,
    one_send,
    one_recv,
    two_send,
    two_recv,
    three_send,
    three_recv,
    out_send,
    out_recv,
    own_qk_sem,
    own_v_sem,
    own_out_sem,
):
    s = lax.axis_index("seq")
    y = lax.axis_index("head")
    z = s // PLANE
    r = s % PLANE
    layers = shards // PLANE
    last = groups - 1
    near = heads * KD

    def y_peer(step):
        return (y + step) % groups

    def r_peer(step):
        return (r + step) % PLANE

    following = (s + 1) % shards
    preceding = (s + shards - 1) % shards
    order = sorted(range(1, groups), key=lambda step: min(step, groups - step))

    barrier = pltpu.get_barrier_semaphore()
    greet = [(s, y_peer(d)) for d in order]
    greet += [(z * PLANE + r_peer(d), y) for d in range(1, PLANE)]
    greet += [(((z + d) % layers) * PLANE + r, y) for d in range(1, layers)]
    for place in greet + [(preceding, last)]:
        pl.semaphore_signal(barrier, inc=1, device_id=place, device_id_type=MESH)

    for g in range(groups):
        own = slice(g * near, (g + 1) * near)
        qk_out[g] = jnp.concatenate([query_ref[:, own], key_ref[:, own]], axis=1)
        taps_qk[g, :KERNEL] = jnp.concatenate([taps_query[:, own], taps_key[:, own]], axis=1)

    @pl.when(y == last)
    def _():
        pl.semaphore_wait(barrier, len(greet) + groups)

    @pl.when(y != last)
    def _():
        pl.semaphore_wait(barrier, len(greet))

    def columns(group, h):
        return pl.ds(pl.multiple_of((group * heads + h) * VD, VD), VD)

    def wide(group):
        return pl.ds(pl.multiple_of(group * heads * VD, heads * VD), heads * VD)

    def remote(src, dst, send, recv, place):
        return pltpu.make_async_remote_copy(
            src_ref=src,
            dst_ref=dst,
            send_sem=send,
            recv_sem=recv,
            device_id=place,
            device_id_type=MESH,
        )

    tail = pl.ds(SPAN - HALO, HALO)

    def send_halo_qk(group):
        return remote(
            qk_out.at[group, tail],
            qk_in.at[0, tail],
            halo_send.at[0, group],
            halo_recv.at[0],
            (following, group),
        )

    def send_halo_v(group):
        return remote(
            v_hbm.at[tail, wide(group)],
            v_halo,
            halo_send.at[1, group],
            halo_recv.at[1],
            (following, group),
        )

    def send_qk(peer, owner):
        return remote(
            qk_out.at[peer], qk_in.at[owner + 1], qk_send.at[peer], qk_recv.at[owner], (s, peer)
        )

    def send_v(h, peer, owner):
        return remote(
            v_hbm.at[:, columns(peer, h)],
            v_in.at[h, owner],
            v_send.at[h, peer],
            v_recv.at[h, owner],
            (s, peer),
        )

    def own_v(h):
        return pltpu.make_async_copy(v_hbm.at[:, columns(y, h)], v_in.at[h, y], own_v_sem.at[h])

    own_qk = pltpu.make_async_copy(qk_out.at[y], qk_in.at[y + 1], own_qk_sem.at[0])
    for d in order:
        send_qk(y_peer(d), y).start()

    @pl.when(y == last)
    def _():
        for group in range(groups):
            send_halo_qk(group).start()
            send_halo_v(group).start()

    own_qk.start()
    for h in range(heads):
        for d in order:
            send_v(h, y_peer(d), y).start()
        own_v(h).start()

    total[...] = jnp.zeros_like(total)
    own_qk.wait()
    for d in order:
        send_qk(y_peer(d), y_peer(d)).wait_recv()
    send_halo_qk(y).wait_recv()

    def expand(n, _):
        keep = jnp.logical_or(n > 0, s > 0)
        before = jnp.where(keep, qk_in[n, SPAN - HALO :].astype(jnp.float32), 0.0)
        qk = convolve(qk_in[n + 1].astype(jnp.float32), before, taps_qk[y, :KERNEL])
        rows = (qk * KD**-0.25).T
        for h in range(heads):
            query = features(rows[h * KD : (h + 1) * KD])
            key = features(rows[near + h * KD : near + (h + 1) * KD])
            query_feat[h, n] = query.T.astype(jnp.bfloat16)
            key_feat[h, n] = key.astype(jnp.bfloat16)
        return 0

    lax.fori_loop(0, groups, expand, 0)
    send_halo_v(y).wait_recv()

    def summarize(h):
        own_v(h).wait()
        for d in order:
            send_v(h, y_peer(d), y_peer(d)).wait_recv()
        taps = taps_v[:, columns(y, h)]
        state = jnp.zeros((FEAT, 2 * VD), jnp.float32)
        for n in range(groups):
            if n == 0:
                before = v_halo[:, pl.ds(pl.multiple_of(h * VD, VD), VD)].astype(jnp.float32)
                before = jnp.where(s > 0, before, 0.0)
            else:
                before = v_in[h, n - 1, SPAN - HALO :].astype(jnp.float32)
            own = convolve(v_in[h, n].astype(jnp.float32), before, taps).astype(jnp.bfloat16)
            value[h, n] = own
            before_state[h, n] = state
            both = jnp.concatenate([own, jnp.ones_like(own)], axis=1)
            state = state + dot(key_feat[h, n], both)
        norm = state[:, VD:].T[:8]
        total[h, :FEAT] = state[:, :VD]
        total[h, FEAT : FEAT + 8] = norm[:, :VD]
        total[h, FEAT + 8 : FEAT + 16, : FEAT - VD] = norm[:, VD:]

    part = total.shape[1] // PLANE

    def piece(index):
        return pl.ds(pl.multiple_of(index * part, 8), part)

    def send_one(h, peer, owner):
        return remote(
            total.at[h, piece(peer)],
            slices.at[h, owner],
            one_send.at[h, peer],
            one_recv.at[h, owner],
            (z * PLANE + peer, y),
        )

    def start_one(h):
        for d in range(1, PLANE):
            send_one(h, r_peer(d), r).start()
        slices[h, r] = total[h, piece(r)]

    def send_two(h, to, owner):
        return remote(
            plane.at[h],
            others.at[h, owner],
            two_send.at[h, to],
            two_recv.at[h, owner],
            (to * PLANE + r, y),
        )

    def start_two(h):
        for d in range(1, PLANE):
            send_one(h, r_peer(d), r_peer(d)).wait_recv()
        running = slices[h, 0]
        for other in range(1, PLANE):
            running = running + slices[h, other]
        plane[h] = running
        for to in range(1, layers):

            @pl.when(z < to)
            def _():
                send_two(h, to, z).start()

    def send_three(h, peer, owner):
        return remote(
            prefixes.at[h, peer],
            carry.at[h, piece(owner)],
            three_send.at[h, peer],
            three_recv.at[h, owner],
            (z * PLANE + peer, y),
        )

    def start_three(h):
        carried[...] = jnp.zeros_like(carried)
        for owner in range(layers - 1):

            @pl.when(owner < z)
            def _():
                send_two(h, z, owner).wait_recv()
                carried[...] += others[h, owner]

        running = carried[...]
        prefixes[h, 0] = running
        for other in range(1, PLANE):
            running = running + slices[h, other - 1]
            prefixes[h, other] = running
        for d in range(1, PLANE):
            send_three(h, r_peer(d), r).start()
        carry[h, piece(r)] = prefixes[h, r]

    causal = lax.broadcasted_iota(jnp.int32, (SPAN, SPAN), 0) >= lax.broadcasted_iota(
        jnp.int32, (SPAN, SPAN), 1
    )

    def attend(h):
        for n in range(groups):
            query = query_feat[h, n]
            scores = jnp.where(causal, dot(query, key_feat[h, n]), 0.0)
            high, low = split(before_state[h, n])
            earlier = dot(query, high) + dot(query, low)
            numer[h, n] = dot(scores.astype(jnp.bfloat16), value[h, n]) + earlier[:, :VD]
            denom[h, n] = jnp.sum(scores, axis=1, keepdims=True) + earlier[:, VD:]

    def send_out(h, peer, owner):
        return remote(
            result.at[h, peer],
            out_ref.at[:, columns(owner, h)],
            out_send.at[h, peer],
            out_recv.at[h, owner],
            (s, peer),
        )

    def own_out(h):
        return pltpu.make_async_copy(
            result.at[h, y], out_ref.at[:, columns(y, h)], own_out_sem.at[h]
        )

    def finish(h):
        for d in range(1, PLANE):
            send_three(h, r_peer(d), r_peer(d)).wait_recv()
        norm = jnp.concatenate(
            [carry[h, FEAT : FEAT + 8], carry[h, FEAT + 8 : FEAT + 16][:, : FEAT - VD]], axis=1
        )
        norm = jnp.broadcast_to(norm[:1], (VD, FEAT)).T
        high, low = split(jnp.concatenate([carry[h, :FEAT], norm], axis=1))
        for d in order + [0]:
            n = y_peer(d)
            query = query_feat[h, n]
            earlier = dot(query, high) + dot(query, low)
            mixed = (numer[h, n] + earlier[:, :VD]) / (denom[h, n] + earlier[:, VD:])
            result[h, n] = mixed.astype(jnp.bfloat16)
            if d:
                send_out(h, n, y).start()
        own_out(h).start()

    summarize(0)
    start_one(0)
    attend(0)
    start_two(0)

    def one_head(h, _):
        summarize(h)
        start_one(h)
        start_three(h - 1)
        attend(h)
        start_two(h)
        finish(h - 1)
        return 0

    lax.fori_loop(1, heads, one_head, 0)
    start_three(heads - 1)
    finish(heads - 1)

    for d in order:
        send_qk(y_peer(d), y).wait_send()

    @pl.when(y == last)
    def _():
        for group in range(groups):
            send_halo_qk(group).wait_send()
            send_halo_v(group).wait_send()

    def drain(h, _):
        for d in order:
            send_v(h, y_peer(d), y).wait_send()
        for d in range(1, PLANE):
            send_one(h, r_peer(d), r).wait_send()
            send_three(h, r_peer(d), r).wait_send()
        for to in range(1, layers):

            @pl.when(z < to)
            def _():
                send_two(h, to, z).wait_send()

        own_out(h).wait()
        for d in order:
            send_out(h, y_peer(d), y).wait_send()
            send_out(h, y_peer(d), y_peer(d)).wait_recv()
        return 0

    lax.fori_loop(0, heads, drain, 0)


def on_device(shards, groups, query_proj, key_proj, value_proj, conv_query, conv_key, conv_value):
    tokens = query_proj.shape[0]
    heads = query_proj.shape[1] // KD // groups
    rows = -(-(FEAT + 16) // (8 * PLANE)) * 8 * PLANE
    part = rows // PLANE
    layers = shards // PLANE
    scratch = pltpu.VMEM
    dma = pltpu.SemaphoreType.DMA
    f32, bf16 = jnp.float32, jnp.bfloat16
    whole = pl.BlockSpec(memory_space=pltpu.VMEM)
    return pl.pallas_call(
        functools.partial(kernel, shards, groups, heads),
        out_shape=jax.ShapeDtypeStruct(value_proj.shape, bf16),
        in_specs=[whole, whole, pl.BlockSpec(memory_space=pl.ANY), whole, whole, whole],
        out_specs=whole,
        scratch_shapes=[
            scratch((groups, tokens, 2 * heads * KD), bf16),
            scratch((groups + 1, tokens, 2 * heads * KD), bf16),
            scratch((heads, groups, tokens, VD), bf16),
            scratch((HALO, heads * VD), bf16),
            scratch((groups, 8, 2 * heads * KD), f32),
            scratch((heads, groups, FEAT, SPAN), bf16),
            scratch((heads, groups, SPAN, FEAT), bf16),
            scratch((heads, groups, SPAN, VD), bf16),
            scratch((heads, groups, FEAT, 2 * VD), f32),
            scratch((heads, groups, SPAN, VD), f32),
            scratch((heads, groups, SPAN, VD), f32),
            scratch((heads, rows, VD), f32),
            scratch((heads, PLANE, part, VD), f32),
            scratch((heads, part, VD), f32),
            scratch((heads, layers, part, VD), f32),
            scratch((part, VD), f32),
            scratch((heads, PLANE, part, VD), f32),
            scratch((heads, rows, VD), f32),
            scratch((heads, groups, tokens, VD), bf16),
            dma((groups,)),
            dma((groups,)),
            dma((heads, groups)),
            dma((heads, groups)),
            dma((2, groups)),
            dma((2,)),
            dma((heads, PLANE)),
            dma((heads, PLANE)),
            dma((heads, layers)),
            dma((heads, layers)),
            dma((heads, PLANE)),
            dma((heads, PLANE)),
            dma((heads, groups)),
            dma((heads, groups)),
            dma((1,)),
            dma((heads,)),
            dma((heads,)),
        ],
        compiler_params=pltpu.CompilerParams(collective_id=0, has_side_effects=True),
    )(query_proj, key_proj, value_proj, conv_query, conv_key, conv_value)


def solution(mesh):
    shards, groups = mesh.shape["seq"], mesh.shape["head"]
    rows = P(("seq", "head"), None)
    return jax.shard_map(
        functools.partial(on_device, shards, groups),
        mesh=mesh,
        in_specs=(rows, rows, rows, P(), P(), P()),
        out_specs=rows,
        check_vma=False,
    )
```

```python
import functools

import jax
import jax.numpy as jnp
from jax import lax
from jax.experimental import pallas as pl
from jax.experimental.pallas import tpu as pltpu
from jax.sharding import PartitionSpec as P

KD = 16
VD = 128
SPAN = 128
KERNEL = 3
HALO = 8
FEAT = 160
PLANE = 8
MESH = pl.DeviceIdType.MESH


def features(rows):
    parts = [rows, rows * rows * (0.5**0.5)]
    for step in range(1, KD // 2):
        parts.append(rows * jnp.concatenate([rows[step:], rows[:step]], axis=0))
    parts.append(rows[: KD // 2] * rows[KD // 2 :])
    index = lax.broadcasted_iota(jnp.int32, (8, rows.shape[1]), 0)
    parts.append(jnp.where(index == 0, 1.0, 0.0).astype(jnp.float32))
    return jnp.concatenate(parts, axis=0)


def convolve(block, before, taps):
    row = lax.broadcasted_iota(jnp.int32, block.shape, 0)
    last = before[HALO - 1 : HALO]
    second = before[HALO - 2 : HALO - 1]
    one = jnp.where(row == 0, last, pltpu.roll(block, 1, 0))
    two = jnp.where(row == 0, second, jnp.where(row == 1, last, pltpu.roll(block, 2, 0)))
    return taps[0:1] * block + taps[1:2] * one + taps[2:3] * two


def split(value):
    high = value.astype(jnp.bfloat16)
    return high, (value - high.astype(jnp.float32)).astype(jnp.bfloat16)


def dot(a, b):
    return jnp.dot(a, b, preferred_element_type=jnp.float32)


def kernel(
    shards,
    groups,
    heads,
    query_ref,
    key_ref,
    v_hbm,
    taps_query,
    taps_key,
    taps_v,
    out_hbm,
    qk_out,
    qk_in,
    v_in,
    v_halo,
    taps_qk,
    key_feat,
    query_feat,
    value,
    before_state,
    numer,
    denom,
    total,
    slices,
    plane,
    others,
    carried,
    prefixes,
    carry,
    result,
    qk_send,
    qk_recv,
    v_send,
    v_recv,
    halo_send,
    halo_recv,
    one_send,
    one_recv,
    two_send,
    two_recv,
    three_send,
    three_recv,
    out_send,
    out_recv,
    own_qk_sem,
    own_v_sem,
    own_out_sem,
):
    s = lax.axis_index("seq")
    y = lax.axis_index("head")
    z = s // PLANE
    r = s % PLANE
    layers = shards // PLANE
    last = groups - 1
    near = heads * KD

    def y_peer(step):
        return (y + step) % groups

    def r_peer(step):
        return (r + step) % PLANE

    following = (s + 1) % shards
    preceding = (s + shards - 1) % shards
    order = sorted(range(1, groups), key=lambda step: min(step, groups - step))

    barrier = pltpu.get_barrier_semaphore()
    greet = [(s, y_peer(d)) for d in order]
    greet += [(z * PLANE + r_peer(d), y) for d in range(1, PLANE)]
    greet += [(((z + d) % layers) * PLANE + r, y) for d in range(1, layers)]
    for place in greet + [(preceding, last)]:
        pl.semaphore_signal(barrier, inc=1, device_id=place, device_id_type=MESH)

    for g in range(groups):
        own = slice(g * near, (g + 1) * near)
        qk_out[g] = jnp.concatenate([query_ref[:, own], key_ref[:, own]], axis=1)
        taps_qk[g, :KERNEL] = jnp.concatenate([taps_query[:, own], taps_key[:, own]], axis=1)

    @pl.when(y == last)
    def _():
        pl.semaphore_wait(barrier, len(greet) + groups)

    @pl.when(y != last)
    def _():
        pl.semaphore_wait(barrier, len(greet))

    def columns(group, h):
        return pl.ds(pl.multiple_of((group * heads + h) * VD, VD), VD)

    def wide(group):
        return pl.ds(pl.multiple_of(group * heads * VD, heads * VD), heads * VD)

    def remote(src, dst, send, recv, place):
        return pltpu.make_async_remote_copy(
            src_ref=src,
            dst_ref=dst,
            send_sem=send,
            recv_sem=recv,
            device_id=place,
            device_id_type=MESH,
        )

    tail = pl.ds(SPAN - HALO, HALO)

    def send_halo_qk(group):
        return remote(
            qk_out.at[group, tail],
            qk_in.at[0, tail],
            halo_send.at[0, group],
            halo_recv.at[0],
            (following, group),
        )

    def send_halo_v(group):
        return remote(
            v_hbm.at[tail, wide(group)],
            v_halo,
            halo_send.at[1, group],
            halo_recv.at[1],
            (following, group),
        )

    def send_qk(peer, owner):
        return remote(
            qk_out.at[peer], qk_in.at[owner + 1], qk_send.at[peer], qk_recv.at[owner], (s, peer)
        )

    def send_v(h, peer, owner):
        return remote(
            v_hbm.at[:, columns(peer, h)],
            v_in.at[h, owner],
            v_send.at[h, peer],
            v_recv.at[h, owner],
            (s, peer),
        )

    def own_v(h):
        return pltpu.make_async_copy(v_hbm.at[:, columns(y, h)], v_in.at[h, y], own_v_sem.at[h])

    own_qk = pltpu.make_async_copy(qk_out.at[y], qk_in.at[y + 1], own_qk_sem.at[0])
    for d in order:
        send_qk(y_peer(d), y).start()

    @pl.when(y == last)
    def _():
        for group in range(groups):
            send_halo_qk(group).start()
            send_halo_v(group).start()

    own_qk.start()
    for h in range(heads):
        for d in order:
            send_v(h, y_peer(d), y).start()
        own_v(h).start()

    total[...] = jnp.zeros_like(total)
    own_qk.wait()
    for d in order:
        send_qk(y_peer(d), y_peer(d)).wait_recv()
    send_halo_qk(y).wait_recv()

    def expand(n, _):
        keep = jnp.logical_or(n > 0, s > 0)
        before = jnp.where(keep, qk_in[n, SPAN - HALO :].astype(jnp.float32), 0.0)
        qk = convolve(qk_in[n + 1].astype(jnp.float32), before, taps_qk[y, :KERNEL])
        rows = (qk * KD**-0.25).T
        for h in range(heads):
            query = features(rows[h * KD : (h + 1) * KD])
            key = features(rows[near + h * KD : near + (h + 1) * KD])
            query_feat[h, n] = query.T.astype(jnp.bfloat16)
            key_feat[h, n] = key.astype(jnp.bfloat16)
        return 0

    lax.fori_loop(0, groups, expand, 0)
    send_halo_v(y).wait_recv()

    def summarize(h):
        own_v(h).wait()
        for d in order:
            send_v(h, y_peer(d), y_peer(d)).wait_recv()
        taps = taps_v[:, columns(y, h)]
        state = jnp.zeros((FEAT, 2 * VD), jnp.float32)
        for n in range(groups):
            if n == 0:
                before = v_halo[:, pl.ds(pl.multiple_of(h * VD, VD), VD)].astype(jnp.float32)
                before = jnp.where(s > 0, before, 0.0)
            else:
                before = v_in[h, n - 1, SPAN - HALO :].astype(jnp.float32)
            own = convolve(v_in[h, n].astype(jnp.float32), before, taps).astype(jnp.bfloat16)
            value[h, n] = own
            before_state[h, n] = state
            both = jnp.concatenate([own, jnp.ones_like(own)], axis=1)
            state = state + dot(key_feat[h, n], both)
        norm = state[:, VD:].T[:8]
        total[h, :FEAT] = state[:, :VD]
        total[h, FEAT : FEAT + 8] = norm[:, :VD]
        total[h, FEAT + 8 : FEAT + 16, : FEAT - VD] = norm[:, VD:]

    part = total.shape[1] // PLANE

    def piece(index):
        return pl.ds(pl.multiple_of(index * part, 8), part)

    def send_one(h, peer, owner):
        return remote(
            total.at[h, piece(peer)],
            slices.at[h, owner],
            one_send.at[h, peer],
            one_recv.at[h, owner],
            (z * PLANE + peer, y),
        )

    def start_one(h):
        for d in range(1, PLANE):
            send_one(h, r_peer(d), r).start()
        slices[h, r] = total[h, piece(r)]

    def send_two(h, to, owner):
        return remote(
            plane.at[h],
            others.at[h, owner],
            two_send.at[h, to],
            two_recv.at[h, owner],
            (to * PLANE + r, y),
        )

    def start_two(h):
        for d in range(1, PLANE):
            send_one(h, r_peer(d), r_peer(d)).wait_recv()
        running = slices[h, 0]
        for other in range(1, PLANE):
            running = running + slices[h, other]
        plane[h] = running
        for to in range(1, layers):

            @pl.when(z < to)
            def _():
                send_two(h, to, z).start()

    def send_three(h, peer, owner):
        return remote(
            prefixes.at[h, peer],
            carry.at[h, piece(owner)],
            three_send.at[h, peer],
            three_recv.at[h, owner],
            (z * PLANE + peer, y),
        )

    def start_three(h):
        carried[...] = jnp.zeros_like(carried)
        for owner in range(layers - 1):

            @pl.when(owner < z)
            def _():
                send_two(h, z, owner).wait_recv()
                carried[...] += others[h, owner]

        running = carried[...]
        prefixes[h, 0] = running
        for other in range(1, PLANE):
            running = running + slices[h, other - 1]
            prefixes[h, other] = running
        for d in range(1, PLANE):
            send_three(h, r_peer(d), r).start()
        carry[h, piece(r)] = prefixes[h, r]

    causal = lax.broadcasted_iota(jnp.int32, (SPAN, SPAN), 0) >= lax.broadcasted_iota(
        jnp.int32, (SPAN, SPAN), 1
    )

    def attend(h):
        for n in range(groups):
            query = query_feat[h, n]
            scores = jnp.where(causal, dot(query, key_feat[h, n]), 0.0)
            high, low = split(before_state[h, n])
            earlier = dot(query, high) + dot(query, low)
            numer[h, n] = dot(scores.astype(jnp.bfloat16), value[h, n]) + earlier[:, :VD]
            denom[h, n] = jnp.sum(scores, axis=1, keepdims=True) + earlier[:, VD:]

    def send_out(h, peer, owner):
        return remote(
            result.at[h, peer],
            out_hbm.at[:, columns(owner, h)],
            out_send.at[h, peer],
            out_recv.at[h, owner],
            (s, peer),
        )

    def own_out(h):
        return pltpu.make_async_copy(
            result.at[h, y], out_hbm.at[:, columns(y, h)], own_out_sem.at[h]
        )

    def finish(h):
        for d in range(1, PLANE):
            send_three(h, r_peer(d), r_peer(d)).wait_recv()
        norm = jnp.concatenate(
            [carry[h, FEAT : FEAT + 8], carry[h, FEAT + 8 : FEAT + 16][:, : FEAT - VD]], axis=1
        )
        norm = jnp.broadcast_to(norm[:1], (VD, FEAT)).T
        high, low = split(jnp.concatenate([carry[h, :FEAT], norm], axis=1))
        for d in order + [0]:
            n = y_peer(d)
            query = query_feat[h, n]
            earlier = dot(query, high) + dot(query, low)
            mixed = (numer[h, n] + earlier[:, :VD]) / (denom[h, n] + earlier[:, VD:])
            result[h, n] = mixed.astype(jnp.bfloat16)
            if d:
                send_out(h, n, y).start()
        own_out(h).start()

    summarize(0)
    start_one(0)
    attend(0)
    start_two(0)

    def one_head(h, _):
        summarize(h)
        start_one(h)
        start_three(h - 1)
        attend(h)
        start_two(h)
        finish(h - 1)
        return 0

    lax.fori_loop(1, heads, one_head, 0)
    start_three(heads - 1)
    finish(heads - 1)

    for d in order:
        send_qk(y_peer(d), y).wait_send()

    @pl.when(y == last)
    def _():
        for group in range(groups):
            send_halo_qk(group).wait_send()
            send_halo_v(group).wait_send()

    def drain(h, _):
        for d in order:
            send_v(h, y_peer(d), y).wait_send()
        for d in range(1, PLANE):
            send_one(h, r_peer(d), r).wait_send()
            send_three(h, r_peer(d), r).wait_send()
        for to in range(1, layers):

            @pl.when(z < to)
            def _():
                send_two(h, to, z).wait_send()

        own_out(h).wait()
        for d in order:
            send_out(h, y_peer(d), y).wait_send()
            send_out(h, y_peer(d), y_peer(d)).wait_recv()
        return 0

    lax.fori_loop(0, heads, drain, 0)


def on_device(shards, groups, query_proj, key_proj, value_proj, conv_query, conv_key, conv_value):
    tokens = query_proj.shape[0]
    heads = query_proj.shape[1] // KD // groups
    rows = -(-(FEAT + 16) // (8 * PLANE)) * 8 * PLANE
    part = rows // PLANE
    layers = shards // PLANE
    scratch = pltpu.VMEM
    dma = pltpu.SemaphoreType.DMA
    f32, bf16 = jnp.float32, jnp.bfloat16
    whole = pl.BlockSpec(memory_space=pltpu.VMEM)
    return pl.pallas_call(
        functools.partial(kernel, shards, groups, heads),
        out_shape=jax.ShapeDtypeStruct(value_proj.shape, bf16),
        in_specs=[whole, whole, pl.BlockSpec(memory_space=pl.ANY), whole, whole, whole],
        out_specs=pl.BlockSpec(memory_space=pl.ANY),
        scratch_shapes=[
            scratch((groups, tokens, 2 * heads * KD), bf16),
            scratch((groups + 1, tokens, 2 * heads * KD), bf16),
            scratch((heads, groups, tokens, VD), bf16),
            scratch((HALO, heads * VD), bf16),
            scratch((groups, 8, 2 * heads * KD), f32),
            scratch((heads, groups, FEAT, SPAN), bf16),
            scratch((heads, groups, SPAN, FEAT), bf16),
            scratch((heads, groups, SPAN, VD), bf16),
            scratch((heads, groups, FEAT, 2 * VD), f32),
            scratch((heads, groups, SPAN, VD), f32),
            scratch((heads, groups, SPAN, VD), f32),
            scratch((heads, rows, VD), f32),
            scratch((heads, PLANE, part, VD), f32),
            scratch((heads, part, VD), f32),
            scratch((heads, layers, part, VD), f32),
            scratch((part, VD), f32),
            scratch((heads, PLANE, part, VD), f32),
            scratch((heads, rows, VD), f32),
            scratch((heads, groups, tokens, VD), bf16),
            dma((groups,)),
            dma((groups,)),
            dma((heads, groups)),
            dma((heads, groups)),
            dma((2, groups)),
            dma((2,)),
            dma((heads, PLANE)),
            dma((heads, PLANE)),
            dma((heads, layers)),
            dma((heads, layers)),
            dma((heads, PLANE)),
            dma((heads, PLANE)),
            dma((heads, groups)),
            dma((heads, groups)),
            dma((1,)),
            dma((heads,)),
            dma((heads,)),
        ],
        compiler_params=pltpu.CompilerParams(collective_id=0, has_side_effects=True),
    )(query_proj, key_proj, value_proj, conv_query, conv_key, conv_value)


def solution(mesh):
    shards, groups = mesh.shape["seq"], mesh.shape["head"]
    rows = P(("seq", "head"), None)
    return jax.shard_map(
        functools.partial(on_device, shards, groups),
        mesh=mesh,
        in_specs=(rows, rows, rows, P(), P(), P()),
        out_specs=rows,
        check_vma=False,
    )
```
